32 devices in a mesh: layer: 2 (over y), row: 4 (over z), col: 4 (over x, core).
Axes of the slice: x: 2, y: 2, z: 4, core: 2. Of those that a mesh axis runs over, the one named last changes fastest.
Arguments:
- leaf_sol: bfloat16 [8, 256, 256], P(('layer', 'col'), 'row'), may hold values from -6 to 6
- lower_blocks: bfloat16 [8192, 1024], P(('layer', 'row'), 'col'), may hold values from -0.1875 to 0.1875
- lower_mask: int32 [32, 4], P(('layer', 'row'), 'col'), may hold values 0 or 1
- upper_blocks: bfloat16 [2048, 4096], P(('layer', 'col'), 'row'), may hold values from -0.125 to 0.125
- upper_mask: int32 [8, 16], P(('layer', 'col'), 'row'), may hold values 0 or 1
- anc_rhs: bfloat16 [4096, 256], P(('row', 'col')), may hold values from -6 to 6
- diag_inv: bfloat16 [4096, 256], P(('row', 'col')), may hold values from -0.375 to 0.375
Outputs:
- new_leaves: bfloat16 [8, 256, 256], P(('layer', 'col'), 'row')
- anc_sol: bfloat16 [4096, 256], P(('row', 'col'))
The draws below stay inside these ranges and needn't reach their ends.
Inputs may be any that keep to these rules, and one draw needn't show every extreme that they name: `lower_mask`: 1 marks a stored block of L. `upper_mask`: 1 marks a stored block of U.
All inputs are finite; a program needn't handle non-finite values.
Results may differ from the reference program's by a relative error of at most 0.0044.
Values may be sent and summed in bfloat16 or wider, within the bound.
A program may use at most 64 MiB of HBM per device.

```python
import jax
import jax.numpy as jnp
from jax import lax

BS = 256
RHS = 256
ANC = 4096
LEAF = 1024
N_LAYER = 2
N_COL = 4


def plant(drawn, stream_key, low, largest):
    longest = drawn.shape.index(max(drawn.shape))
    spots = []
    for shift in (0, 1):
        where = [jax.random.randint(jax.random.fold_in(stream_key, axis), (), 0, length) for axis, length in enumerate(drawn.shape)]
        where[longest] = (where[longest] + shift) % drawn.shape[longest]
        spots.append(tuple(where))
    return drawn.at[spots[0]].set(low).at[spots[1]].set(largest)


def steps_of(stream_key, dims, pieces, smallest, top_value):
    def one(position, blocks):
        steps = jax.random.uniform(jax.random.fold_in(jax.random.fold_in(stream_key, 6), position), (blocks,), jnp.float32, smallest / len(pieces), top_value / len(pieces))
        return jnp.repeat(jnp.exp(steps), dims[position] // blocks).reshape((-1,) + (1,) * (len(dims) - position - 1))

    level = one(*pieces[0])
    for cut in pieces[1:]:
        level = level * one(*cut)
    return level


def gaussian(own_key, dims, width, limit, pieces=(), kind=jnp.bfloat16):
    factor_of = steps_of(own_key, dims, pieces, -0.22, 0.18) if pieces else 1.0
    entries = jax.random.normal(own_key, dims, jnp.float32) * width * factor_of
    return jnp.minimum(jnp.maximum(entries, -limit), limit).astype(kind)


def setup_inputs(seed: int = 0) -> dict:
    arg_keys = jax.random.split(jax.random.key(seed), 8)
    return {
        "leaf_sol": gaussian(arg_keys[0], (N_LAYER * N_COL, LEAF // N_COL, RHS), 1.0, 6.0, ((0, 8), (1, 4))),
        "lower_blocks": gaussian(arg_keys[1], (N_LAYER * ANC, LEAF), (LEAF * N_LAYER // 2) ** -0.5, 0.1875, ((0, 8), (1, 4))),
        "lower_mask": plant((jax.random.randint(arg_keys[2], (N_LAYER * ANC // BS, LEAF // BS), 0, 2) < 1).astype(jnp.int32), jax.random.fold_in(arg_keys[2], 1), 0, 1),
        "upper_blocks": gaussian(arg_keys[3], (N_LAYER * LEAF, ANC), (ANC // 2) ** -0.5, 0.125, ((0, 8), (1, 4))),
        "upper_mask": plant((jax.random.randint(arg_keys[4], (N_LAYER * LEAF // BS, ANC // BS), 0, 2) < 1).astype(jnp.int32), jax.random.fold_in(arg_keys[4], 1), 0, 1),
        "anc_rhs": gaussian(arg_keys[5], (ANC, RHS), 1.0, 6.0, ((0, 16),)),
        "diag_inv": gaussian(arg_keys[6], (ANC, BS), BS ** -0.5, 0.375, ((0, 16),)),
    }


def expand(mask, block):
    first, second = mask.shape
    full = jnp.broadcast_to(mask[:, None, :, None], (first, block, second, block))
    return full.reshape(first * block, second * block)


def reference(leaf_sol, lower_blocks, lower_mask, upper_blocks, upper_mask, anc_rhs, diag_inv):
    anc_blocks = ANC // BS
    leaf_count = LEAF // BS
    leaf_all = leaf_sol.reshape(N_LAYER, LEAF, RHS)

    def lower_layer(layer_id):
        band = lax.dynamic_slice_in_dim(lower_blocks, layer_id * ANC, ANC, 0)
        marks = lax.dynamic_slice_in_dim(lower_mask, layer_id * anc_blocks, anc_blocks, 0)
        masked = band * expand(marks, BS).astype(jnp.bfloat16)
        solved = lax.dynamic_index_in_dim(leaf_all, layer_id, 0, keepdims=False)
        return jnp.dot(masked, solved, preferred_element_type=jnp.float32)

    layers = jnp.arange(N_LAYER, dtype=jnp.int32)
    summed = jnp.sum(lax.map(lower_layer, layers), axis=0)
    remain = anc_rhs.astype(jnp.float32) - summed
    inverse = diag_inv.reshape(anc_blocks, BS, BS).astype(jnp.float32)
    solved_anc = jnp.einsum("kij,kjr->kir", inverse, remain.reshape(anc_blocks, BS, RHS),
                            precision=lax.Precision.HIGHEST)
    anc_sol = solved_anc.reshape(ANC, RHS).astype(jnp.bfloat16)

    def upper_layer(layer_id):
        band = lax.dynamic_slice_in_dim(upper_blocks, layer_id * LEAF, LEAF, 0)
        marks = lax.dynamic_slice_in_dim(upper_mask, layer_id * leaf_count, leaf_count, 0)
        masked = band * expand(marks, BS).astype(jnp.bfloat16)
        correct = jnp.dot(masked, anc_sol, preferred_element_type=jnp.float32)
        solved = lax.dynamic_index_in_dim(leaf_all, layer_id, 0, keepdims=False)
        return (solved.astype(jnp.float32) - correct).astype(jnp.bfloat16)

    new_leaves = lax.map(upper_layer, layers).reshape(leaf_sol.shape)
    return new_leaves, anc_sol
```

```python
import functools

import jax
import jax.numpy as jnp
from jax import lax
from jax.experimental import pallas as pl
from jax.experimental.pallas import tpu as pltpu
from jax.sharding import PartitionSpec as P

MESH = pl.DeviceIdType.MESH


def dot_last(a, b):
    return lax.dot_general(a, b, (((1,), (1,)), ((), ())), preferred_element_type=jnp.float32)


def kernel(
    n_layer, n_row, n_col,
    leaf, lower, lower_mask, upper, upper_mask, rhs, inv,
    new_leaves, anc_out,
    leaf_v, lower_v, upper_v, rhs_v, inv_v, x_all, x_t, rhs_t, part, part_in, anc_t, fold, fold_in,
    local_sem, x_send, x_recv, part_send, part_recv, anc_send, anc_recv, fold_send, fold_recv,
):
    layer = lax.axis_index("layer")
    row = lax.axis_index("row")
    col = lax.axis_index("col")
    block = inv_v.shape[0]
    width = rhs_v.shape[1]
    share = width // n_layer
    strip = leaf_v.shape[0]
    depth = x_all.shape[0] * strip
    group = [(dl, dc) for dl in range(n_layer) for dc in range(n_col) if (dl, dc) != (0, 0)]

    loads = [
        pltpu.make_async_copy(source, target, local_sem.at[index])
        for index, (source, target) in enumerate(
            ((leaf.at[0], leaf_v), (lower, lower_v), (rhs, rhs_v), (inv, inv_v), (upper, upper_v))
        )
    ]
    for load in loads:
        load.start()

    barrier = pltpu.get_barrier_semaphore()
    for dr in range(1, n_row):
        pl.semaphore_signal(barrier, inc=1, device_id=(layer, lax.rem(row + dr, n_row), col), device_id_type=MESH)
    for dl, dc in group:
        pl.semaphore_signal(
            barrier, inc=1,
            device_id=(lax.rem(layer + dl, n_layer), row, lax.rem(col + dc, n_col)), device_id_type=MESH,
        )
    pl.semaphore_wait(barrier, n_row - 1 + len(group))

    def x_copy(to_row, from_row):
        return pltpu.make_async_remote_copy(
            src_ref=leaf.at[0], dst_ref=x_all.at[from_row],
            send_sem=x_send.at[to_row], recv_sem=x_recv.at[from_row],
            device_id=(layer, to_row, col), device_id_type=MESH,
        )

    for dr in range(1, n_row):
        x_copy(lax.rem(row + dr, n_row), row).start()
    loads[0].wait()
    x_all[row] = leaf_v[...]
    loads[2].wait()
    rhs_t[...] = rhs_v[...].astype(jnp.float32).T
    loads[1].wait()
    loads[3].wait()
    for dr in range(1, n_row):
        x_copy(row, lax.rem(row + dr, n_row)).wait_recv()
    for k in range(depth // block):
        strips = block // strip
        x_t[k] = x_all[k * strips:(k + 1) * strips].reshape(block, width).T

    def part_copy(source, to_layer, to_col, from_layer, from_col):
        return pltpu.make_async_remote_copy(
            src_ref=source, dst_ref=part_in.at[from_layer * n_col + from_col],
            send_sem=part_send.at[to_layer * n_col + to_col],
            recv_sem=part_recv.at[from_layer * n_col + from_col],
            device_id=(to_layer, row, to_col), device_id_type=MESH,
        )

    own = None
    for dc in list(range(1, n_col)) + [0]:
        to_col = lax.rem(col + dc, n_col)
        total = None
        for k in range(depth // block):
            rows = lower_v[pl.ds(pl.multiple_of(to_col * block, block), block), k * block:(k + 1) * block]
            term = dot_last(x_t[k], rows) * lower_mask[k, to_col].astype(jnp.float32)
            total = term if total is None else total + term
        part[to_col] = total.astype(jnp.bfloat16)
        for dl in list(range(1, n_layer)) + [0]:
            to_layer = lax.rem(layer + dl, n_layer)
            if (dl, dc) != (0, 0):
                part_copy(
                    part.at[to_col, pl.ds(pl.multiple_of(to_layer * share, share), share)],
                    to_layer, to_col, layer, col,
                ).start()

    mine = pl.ds(pl.multiple_of(layer * share, share), share)
    remain = rhs_t[mine, :] - part[col, mine, :].astype(jnp.float32)
    for dl, dc in group:
        from_layer, from_col = lax.rem(layer + dl, n_layer), lax.rem(col + dc, n_col)
        part_copy(part.at[0, pl.ds(0, share)], layer, col, from_layer, from_col).wait_recv()
        remain = remain - part_in[from_layer * n_col + from_col].astype(jnp.float32)
    inverse = inv_v[...]
    high = remain.astype(jnp.bfloat16)
    rest = remain - high.astype(jnp.float32)
    middle = rest.astype(jnp.bfloat16)
    low = (rest - middle.astype(jnp.float32)).astype(jnp.bfloat16)
    solved = dot_last(high, inverse) + (dot_last(middle, inverse) + dot_last(low, inverse))
    anc_t[col, mine, :] = solved.astype(jnp.bfloat16)

    def anc_copy(to_layer, to_col, from_layer, from_col):
        place = anc_t.at[from_col, pl.ds(pl.multiple_of(from_layer * share, share), share)]
        return pltpu.make_async_remote_copy(
            src_ref=place, dst_ref=place,
            send_sem=anc_send.at[to_layer * n_col + to_col],
            recv_sem=anc_recv.at[from_layer * n_col + from_col],
            device_id=(to_layer, row, to_col), device_id_type=MESH,
        )

    for dl, dc in reversed(group):
        anc_copy(lax.rem(layer + dl, n_layer), lax.rem(col + dc, n_col), layer, col).start()

    loads[4].wait()
    blocks_down = upper_v.shape[0] // block
    totals = [None] * blocks_down
    for dc in range(n_col):
        from_col = lax.rem(col + dc, n_col)
        for dl in range(n_layer):
            if (dl, dc) != (0, 0):
                anc_copy(layer, col, lax.rem(layer + dl, n_layer), from_col).wait_recv()
        for i in range(blocks_down):
            tile = upper_v[i * block:(i + 1) * block, pl.ds(pl.multiple_of(from_col * block, block), block)]
            term = dot_last(tile, anc_t[from_col]) * upper_mask[i, from_col].astype(jnp.float32)
            totals[i] = term if totals[i] is None else totals[i] + term
    strips = block // strip
    for i in range(blocks_down):
        fold[i * strips:(i + 1) * strips] = totals[i].astype(jnp.bfloat16).reshape(strips, strip, width)

    def fold_copy(to_row, from_row):
        return pltpu.make_async_remote_copy(
            src_ref=fold.at[to_row], dst_ref=fold_in.at[from_row],
            send_sem=fold_send.at[to_row], recv_sem=fold_recv.at[from_row],
            device_id=(layer, to_row, col), device_id_type=MESH,
        )

    for dr in range(1, n_row):
        fold_copy(lax.rem(row + dr, n_row), row).start()
    anc_out[...] = anc_t[col].T
    correct = fold[row].astype(jnp.float32)
    for dr in range(1, n_row):
        from_row = lax.rem(row + dr, n_row)
        fold_copy(row, from_row).wait_recv()
        correct = correct + fold_in[from_row].astype(jnp.float32)
    new_leaves[0] = (leaf_v[...].astype(jnp.float32) - correct).astype(jnp.bfloat16)

    for dr in range(1, n_row):
        x_copy(lax.rem(row + dr, n_row), row).wait_send()
        fold_copy(lax.rem(row + dr, n_row), row).wait_send()
    for dl, dc in group:
        to_layer, to_col = lax.rem(layer + dl, n_layer), lax.rem(col + dc, n_col)
        part_copy(part.at[0, pl.ds(0, share)], to_layer, to_col, layer, col).wait_send()
        anc_copy(to_layer, to_col, layer, col).wait_send()


def shards(n_layer, n_row, n_col, leaf_sol, lower_blocks, lower_mask, upper_blocks, upper_mask, anc_rhs, diag_inv):
    block = diag_inv.shape[1]
    width = leaf_sol.shape[2]
    strip = leaf_sol.shape[1]
    share = width // n_layer
    bf16 = jnp.bfloat16
    dma = pltpu.SemaphoreType.DMA
    anywhere = pl.BlockSpec(memory_space=pl.ANY)
    scalars = pl.BlockSpec(memory_space=pltpu.SMEM)
    vmem = pl.BlockSpec(memory_space=pltpu.VMEM)
    devices = n_layer * n_col
    return pl.pallas_call(
        functools.partial(kernel, n_layer, n_row, n_col),
        out_shape=(
            jax.ShapeDtypeStruct(leaf_sol.shape, bf16),
            jax.ShapeDtypeStruct(anc_rhs.shape, bf16),
        ),
        in_specs=[anywhere, anywhere, scalars, anywhere, scalars, anywhere, anywhere],
        out_specs=(vmem, vmem),
        scratch_shapes=[
            pltpu.VMEM((strip, width), bf16),
            pltpu.VMEM(lower_blocks.shape, bf16),
            pltpu.VMEM(upper_blocks.shape, bf16),
            pltpu.VMEM(anc_rhs.shape, bf16),
            pltpu.VMEM(diag_inv.shape, bf16),
            pltpu.VMEM((n_row, strip, width), bf16),
            pltpu.VMEM((n_row * strip // block, width, block), bf16),
            pltpu.VMEM((width, block), jnp.float32),
            pltpu.VMEM((n_col, width, block), bf16),
            pltpu.VMEM((devices, share, block), bf16),
            pltpu.VMEM((n_col, width, block), bf16),
            pltpu.VMEM((n_row, strip, width), bf16),
            pltpu.VMEM((n_row, strip, width), bf16),
            dma((5,)),
            dma((n_row,)), dma((n_row,)),
            dma((devices,)), dma((devices,)),
            dma((devices,)), dma((devices,)),
            dma((n_row,)), dma((n_row,)),
        ],
        compiler_params=pltpu.CompilerParams(collective_id=0, has_side_effects=True),
    )(leaf_sol, lower_blocks, lower_mask.T, upper_blocks, upper_mask, anc_rhs, diag_inv)


def solution(mesh):
    in_specs = (
        P(("layer", "col"), "row", None),
        P(("layer", "row"), "col"),
        P(("layer", "row"), "col"),
        P(("layer", "col"), "row"),
        P(("layer", "col"), "row"),
        P(("row", "col"), None),
        P(("row", "col"), None),
    )
    out_specs = (P(("layer", "col"), "row", None), P(("row", "col"), None))
    body = functools.partial(shards, mesh.shape["layer"], mesh.shape["row"], mesh.shape["col"])
    return jax.shard_map(body, mesh=mesh, in_specs=in_specs, out_specs=out_specs, check_vma=False)
```

```python
import functools

import jax
import jax.numpy as jnp
from jax import lax
from jax.experimental import pallas as pl
from jax.experimental.pallas import tpu as pltpu
from jax.sharding import PartitionSpec as P

MESH = pl.DeviceIdType.MESH


def dot_last(a, b):
    return lax.dot_general(a, b, (((1,), (1,)), ((), ())), preferred_element_type=jnp.float32)


def kernel(
    n_layer, n_row, n_col, chunks,
    leaf, lower, lower_mask, upper, upper_mask, rhs, inv,
    new_leaves, anc_out,
    leaf_v, lower_v, upper_v, rhs_v, inv_v, x_all, x_t, rhs_t,
    pair_out, pair_in, held, part, part_in, anc_t, fold, fold_in,
    local_sem, x_send, x_recv, pair_send, pair_recv, part_send, part_recv,
    anc_send, pass_send, anc_recv, fold_send, fold_recv,
):
    layer = lax.axis_index("layer")
    row = lax.axis_index("row")
    col = lax.axis_index("col")
    halves = n_col // 2
    half, side = col // 2, lax.rem(col, 2)
    other = 1 - side
    partner = half * 2 + other
    block = inv_v.shape[0]
    width = rhs_v.shape[1]
    span = width // chunks
    share = span // n_layer
    strip = leaf_v.shape[0]
    depth = x_all.shape[0] * strip
    devices = n_layer * n_col
    group = [(dl, dh) for dl in range(n_layer) for dh in range(halves) if (dl, dh) != (0, 0)]

    def peer(dl, dh):
        return lax.rem(layer + dl, n_layer), lax.rem(half + dh, halves) * 2 + side

    loads = [
        pltpu.make_async_copy(source, target, local_sem.at[index])
        for index, (source, target) in enumerate(
            ((leaf.at[0], leaf_v), (lower, lower_v), (rhs, rhs_v), (inv, inv_v), (upper, upper_v))
        )
    ]
    for load in loads:
        load.start()

    barrier = pltpu.get_barrier_semaphore()
    for dr in reversed(range(1, n_row)):
        pl.semaphore_signal(barrier, inc=1, device_id=(layer, lax.rem(row + dr, n_row), col), device_id_type=MESH)
    for dl, dh in group:
        to_layer, to_col = peer(dl, dh)
        pl.semaphore_signal(barrier, inc=1, device_id=(to_layer, row, to_col), device_id_type=MESH)
    pl.semaphore_signal(barrier, inc=1, device_id=(layer, row, partner), device_id_type=MESH)
    pl.semaphore_wait(barrier, n_row + len(group))

    def x_copy(to_row, from_row):
        return pltpu.make_async_remote_copy(
            src_ref=leaf.at[0], dst_ref=x_all.at[from_row],
            send_sem=x_send.at[to_row], recv_sem=x_recv.at[from_row],
            device_id=(layer, to_row, col), device_id_type=MESH,
        )

    for dr in range(1, n_row):
        x_copy(lax.rem(row + dr, n_row), row).start()
    loads[0].wait()
    x_all[row] = leaf_v[...]
    loads[2].wait()
    rhs_t[...] = rhs_v[...].astype(jnp.float32).T
    loads[1].wait()
    loads[3].wait()
    loads[4].wait()
    for dr in range(1, n_row):
        x_copy(row, lax.rem(row + dr, n_row)).wait_recv()
    strips = block // strip
    for k in range(depth // block):
        x_t[k] = x_all[k * strips:(k + 1) * strips].reshape(block, width).T

    def partial_sum(j, to_col):
        total = None
        for k in range(depth // block):
            rows = lower_v[pl.ds(pl.multiple_of(to_col * block, block), block), k * block:(k + 1) * block]
            term = dot_last(x_t[k, j * span:(j + 1) * span], rows) * lower_mask[k, to_col].astype(jnp.float32)
            total = term if total is None else total + term
        return total

    def pair_copy(j, h):
        return pltpu.make_async_remote_copy(
            src_ref=pair_out.at[j, h], dst_ref=pair_in.at[j, h],
            send_sem=pair_send.at[j * halves + h], recv_sem=pair_recv.at[j * halves + h],
            device_id=(layer, row, partner), device_id_type=MESH,
        )

    for j in range(chunks):
        for h in range(halves):
            pair_out[j, h] = partial_sum(j, h * 2 + other).astype(jnp.bfloat16)
            pair_copy(j, h).start()
        for h in range(halves):
            held[j, h] = partial_sum(j, h * 2 + side)

    def inside(index):
        return pl.ds(pl.multiple_of(index * share, share), share)

    def part_copy(j, to_layer, to_col, from_layer, from_col):
        return pltpu.make_async_remote_copy(
            src_ref=part.at[j, to_col // 2, inside(to_layer)],
            dst_ref=part_in.at[j, from_layer * n_col + from_col],
            send_sem=part_send.at[j * devices + to_layer * n_col + to_col],
            recv_sem=part_recv.at[j * devices + from_layer * n_col + from_col],
            device_id=(to_layer, row, to_col), device_id_type=MESH,
        )

    for j in range(chunks):
        for h in range(halves):
            pair_copy(j, h).wait_recv()
            total = held[j, h] + pair_in[j, h].astype(jnp.float32)
            held[j, h] = total
            part[j, h] = total.astype(jnp.bfloat16)
        for dl, dh in reversed(group):
            part_copy(j, *peer(dl, dh), layer, col).start()

    def anc_place(j, from_layer, from_col):
        return anc_t.at[j, from_col, inside(from_layer)]

    def anc_copy(j, to_layer, to_col, from_layer, from_col):
        place = anc_place(j, from_layer, from_col)
        return pltpu.make_async_remote_copy(
            src_ref=place, dst_ref=place,
            send_sem=anc_send.at[j * devices + to_layer * n_col + to_col],
            recv_sem=anc_recv.at[j * devices + from_layer * n_col + from_col],
            device_id=(to_layer, row, to_col), device_id_type=MESH,
        )

    def pass_copy(j, from_layer, from_col):
        place = anc_place(j, from_layer, from_col)
        return pltpu.make_async_remote_copy(
            src_ref=place, dst_ref=place,
            send_sem=pass_send.at[j * devices + from_layer * n_col + from_col],
            recv_sem=anc_recv.at[j * devices + from_layer * n_col + from_col],
            device_id=(layer, row, partner), device_id_type=MESH,
        )

    inverse = inv_v[...]
    for j in range(chunks):
        remain = rhs_t[pl.ds(pl.multiple_of(j * span + layer * share, share), share), :] - held[j, half, inside(layer)]
        for dl, dh in group:
            from_layer, from_col = peer(dl, dh)
            part_copy(j, layer, col, from_layer, from_col).wait_recv()
            remain = remain - part_in[j, from_layer * n_col + from_col].astype(jnp.float32)
        high = remain.astype(jnp.bfloat16)
        rest = remain - high.astype(jnp.float32)
        middle = rest.astype(jnp.bfloat16)
        low = (rest - middle.astype(jnp.float32)).astype(jnp.bfloat16)
        solved = dot_last(high, inverse) + (dot_last(middle, inverse) + dot_last(low, inverse))
        anc_t[j, col, inside(layer)] = solved.astype(jnp.bfloat16)
        for dl, dh in reversed(group):
            anc_copy(j, *peer(dl, dh), layer, col).start()
        pass_copy(j, layer, col).start()

    def fold_copy(j, to_row, from_row):
        return pltpu.make_async_remote_copy(
            src_ref=fold.at[j, to_row], dst_ref=fold_in.at[j, from_row],
            send_sem=fold_send.at[j * n_row + to_row], recv_sem=fold_recv.at[j * n_row + from_row],
            device_id=(layer, to_row, col), device_id_type=MESH,
        )

    blocks_down = upper_v.shape[0] // block
    for j in range(chunks):
        for dl, dh in group:
            from_layer, from_col = peer(dl, dh)
            anc_copy(j, layer, col, from_layer, from_col).wait_recv()
            pass_copy(j, from_layer, from_col).start()
        totals = [None] * blocks_down
        for parity in (side, other):
            for dh in range(halves):
                from_col = lax.rem(half + dh, halves) * 2 + parity
                if parity is other:
                    for from_layer in range(n_layer):
                        pass_copy(j, from_layer, from_col).wait_recv()
                for i in range(blocks_down):
                    tile = upper_v[i * block:(i + 1) * block, pl.ds(pl.multiple_of(from_col * block, block), block)]
                    term = dot_last(tile, anc_t[j, from_col]) * upper_mask[i, from_col].astype(jnp.float32)
                    totals[i] = term if totals[i] is None else totals[i] + term
        for i in range(blocks_down):
            fold[j, i * strips:(i + 1) * strips] = totals[i].astype(jnp.bfloat16).reshape(strips, strip, span)
        for dr in range(1, n_row):
            fold_copy(j, lax.rem(row + dr, n_row), row).start()

    for j in range(chunks):
        anc_out[:, j * span:(j + 1) * span] = anc_t[j, col].T
    for j in range(chunks):
        correct = fold[j, row].astype(jnp.float32)
        for dr in range(1, n_row):
            from_row = lax.rem(row + dr, n_row)
            fold_copy(j, row, from_row).wait_recv()
            correct = correct + fold_in[j, from_row].astype(jnp.float32)
        columns = slice(j * span, (j + 1) * span)
        new_leaves[0, :, columns] = (leaf_v[:, columns].astype(jnp.float32) - correct).astype(jnp.bfloat16)

    for dr in range(1, n_row):
        x_copy(lax.rem(row + dr, n_row), row).wait_send()
        for j in range(chunks):
            fold_copy(j, lax.rem(row + dr, n_row), row).wait_send()
    for j in range(chunks):
        for h in range(halves):
            pair_copy(j, h).wait_send()
        pass_copy(j, layer, col).wait_send()
        for dl, dh in group:
            to_layer, to_col = peer(dl, dh)
            part_copy(j, to_layer, to_col, layer, col).wait_send()
            anc_copy(j, to_layer, to_col, layer, col).wait_send()
            pass_copy(j, to_layer, to_col).wait_send()


def finish(leaves, anc, leaves_out, anc_out):
    leaves_out[...] = leaves[...]
    anc_out[...] = anc[...]


def shards(n_layer, n_row, n_col, leaf_sol, lower_blocks, lower_mask, upper_blocks, upper_mask, anc_rhs, diag_inv):
    block = diag_inv.shape[1]
    width = leaf_sol.shape[2]
    strip = leaf_sol.shape[1]
    chunks = 2
    span = width // chunks
    share = span // n_layer
    halves = n_col // 2
    bf16, f32 = jnp.bfloat16, jnp.float32
    anywhere = pl.BlockSpec(memory_space=pltpu.HBM)
    scalars = pl.BlockSpec(memory_space=pltpu.SMEM)
    vmem = pl.BlockSpec(memory_space=pltpu.VMEM)
    devices = n_layer * n_col
    dma = lambda *sizes: [pltpu.SemaphoreType.DMA((size,)) for size in sizes]
    out_shape = (
        jax.ShapeDtypeStruct(leaf_sol.shape, bf16),
        jax.ShapeDtypeStruct(anc_rhs.shape, bf16),
    )
    results = pl.pallas_call(
        functools.partial(kernel, n_layer, n_row, n_col, chunks),
        out_shape=out_shape,
        in_specs=[anywhere, anywhere, scalars, anywhere, scalars, anywhere, anywhere],
        out_specs=(vmem, vmem),
        scratch_shapes=[
            pltpu.VMEM((strip, width), bf16),
            pltpu.VMEM(lower_blocks.shape, bf16),
            pltpu.VMEM(upper_blocks.shape, bf16),
            pltpu.VMEM(anc_rhs.shape, bf16),
            pltpu.VMEM(diag_inv.shape, bf16),
            pltpu.VMEM((n_row, strip, width), bf16),
            pltpu.VMEM((n_row * strip // block, width, block), bf16),
            pltpu.VMEM((width, block), f32),
            pltpu.VMEM((chunks, halves, span, block), bf16),
            pltpu.VMEM((chunks, halves, span, block), bf16),
            pltpu.VMEM((chunks, halves, span, block), f32),
            pltpu.VMEM((chunks, halves, span, block), bf16),
            pltpu.VMEM((chunks, devices, share, block), bf16),
            pltpu.VMEM((chunks, n_col, span, block), bf16),
            pltpu.VMEM((chunks, n_row, strip, span), bf16),
            pltpu.VMEM((chunks, n_row, strip, span), bf16),
            *dma(
                5, n_row, n_row, chunks * halves, chunks * halves,
                *[chunks * devices] * 5, chunks * n_row, chunks * n_row,
            ),
        ],
        compiler_params=pltpu.CompilerParams(
            collective_id=0, has_side_effects=True,
        ),
    )(leaf_sol, lower_blocks, lower_mask.T, upper_blocks, upper_mask, anc_rhs, diag_inv)
    return pl.pallas_call(finish, out_shape=out_shape, in_specs=[vmem] * 2, out_specs=(vmem, vmem))(*results)


def solution(mesh):
    in_specs = (
        P(("layer", "col"), "row", None),
        P(("layer", "row"), "col"),
        P(("layer", "row"), "col"),
        P(("layer", "col"), "row"),
        P(("layer", "col"), "row"),
        P(("row", "col"), None),
        P(("row", "col"), None),
    )
    out_specs = (P(("layer", "col"), "row", None), P(("row", "col"), None))
    body = functools.partial(shards, mesh.shape["layer"], mesh.shape["row"], mesh.shape["col"])
    return jax.shard_map(body, mesh=mesh, in_specs=in_specs, out_specs=out_specs, check_vma=False)
```

```python
import functools

import jax
import jax.numpy as jnp
from jax import lax
from jax.experimental import pallas as pl
from jax.experimental.pallas import tpu as pltpu
from jax.sharding import PartitionSpec as P

MESH = pl.DeviceIdType.MESH


def dot_last(a, b):
    return lax.dot_general(a, b, (((1,), (1,)), ((), ())), preferred_element_type=jnp.float32)


def kernel(
    n_layer, n_row, n_col, chunks,
    leaf, lower, lower_mask, upper, upper_mask, rhs, inv,
    new_leaves, anc_out,
    leaf_v, lower_v, upper_v, rhs_v, inv_v, x_all, x_t, rhs_t,
    pair_out, pair_in, held, part, part_in, anc_t, fold, fold_in,
    local_sem, x_send, x_recv, pair_send, pair_recv, part_send, part_recv,
    anc_send, pass_send, anc_recv, fold_send, fold_recv,
):
    layer = lax.axis_index("layer")
    row = lax.axis_index("row")
    col = lax.axis_index("col")
    halves = n_col // 2
    half, side = col // 2, lax.rem(col, 2)
    other = 1 - side
    partner = half * 2 + other
    block = inv_v.shape[0]
    width = rhs_v.shape[1]
    span = width // chunks
    share = span // n_layer
    strip = leaf_v.shape[0]
    depth = n_row * strip
    devices = n_layer * n_col
    group = [(dl, dh) for dl in range(n_layer) for dh in range(halves) if (dl, dh) != (0, 0)]

    def peer(dl, dh):
        return lax.rem(layer + dl, n_layer), lax.rem(half + dh, halves) * 2 + side

    loads = [
        pltpu.make_async_copy(source, target, local_sem.at[index])
        for index, (source, target) in enumerate(
            ((leaf.at[0], leaf_v), (lower, lower_v), (rhs, rhs_v), (inv, inv_v), (upper, upper_v))
        )
    ]
    for load in loads:
        load.start()

    barrier = pltpu.get_barrier_semaphore()
    for dr in reversed(range(1, n_row)):
        pl.semaphore_signal(barrier, inc=1, device_id=(layer, lax.rem(row + dr, n_row), col), device_id_type=MESH)
    for dl, dh in group:
        to_layer, to_col = peer(dl, dh)
        pl.semaphore_signal(barrier, inc=1, device_id=(to_layer, row, to_col), device_id_type=MESH)
    pl.semaphore_signal(barrier, inc=1, device_id=(layer, row, partner), device_id_type=MESH)
    pl.semaphore_wait(barrier, n_row + len(group))

    def x_copy(j, to_row, from_row):
        return pltpu.make_async_remote_copy(
            src_ref=leaf.at[0, :, pl.ds(j * span, span)], dst_ref=x_all.at[j, from_row],
            send_sem=x_send.at[j * n_row + to_row], recv_sem=x_recv.at[j * n_row + from_row],
            device_id=(layer, to_row, col), device_id_type=MESH,
        )

    for j in range(chunks):
        for dr in range(1, n_row):
            x_copy(j, lax.rem(row + dr, n_row), row).start()
    loads[0].wait()
    for j in range(chunks):
        x_all[j, row] = leaf_v[:, j * span:(j + 1) * span]
    loads[2].wait()
    rhs_t[...] = rhs_v[...].astype(jnp.float32).T
    loads[1].wait()
    loads[3].wait()
    loads[4].wait()
    strips = block // strip

    def partial_sum(j, to_col):
        total = None
        for k in range(depth // block):
            rows = lower_v[pl.ds(pl.multiple_of(to_col * block, block), block), k * block:(k + 1) * block]
            term = dot_last(x_t[j, k], rows) * lower_mask[k, to_col].astype(jnp.float32)
            total = term if total is None else total + term
        return total

    def pair_copy(j, h):
        return pltpu.make_async_remote_copy(
            src_ref=pair_out.at[j, h], dst_ref=pair_in.at[j, h],
            send_sem=pair_send.at[j * halves + h], recv_sem=pair_recv.at[j * halves + h],
            device_id=(layer, row, partner), device_id_type=MESH,
        )

    def inside(index):
        return pl.ds(pl.multiple_of(index * share, share), share)

    def part_copy(j, to_layer, to_col, from_layer, from_col):
        return pltpu.make_async_remote_copy(
            src_ref=part.at[j, to_col // 2, inside(to_layer)],
            dst_ref=part_in.at[j, from_layer * n_col + from_col],
            send_sem=part_send.at[j * devices + to_layer * n_col + to_col],
            recv_sem=part_recv.at[j * devices + from_layer * n_col + from_col],
            device_id=(to_layer, row, to_col), device_id_type=MESH,
        )

    for j in range(chunks):
        for dr in range(1, n_row):
            x_copy(j, row, lax.rem(row + dr, n_row)).wait_recv()
        for k in range(depth // block):
            x_t[j, k] = x_all[j, k * strips:(k + 1) * strips].reshape(block, span).T
        for h in range(halves):
            pair_out[j, h] = partial_sum(j, h * 2 + other).astype(jnp.bfloat16)
            pair_copy(j, h).start()
        for h in range(halves):
            held[j, h] = partial_sum(j, h * 2 + side)
        for h in range(halves):
            pair_copy(j, h).wait_recv()
            total = held[j, h] + pair_in[j, h].astype(jnp.float32)
            held[j, h] = total
            part[j, h] = total.astype(jnp.bfloat16)
        for dl, dh in reversed(group):
            part_copy(j, *peer(dl, dh), layer, col).start()

    def anc_place(j, from_layer, from_col):
        return anc_t.at[j, from_col, inside(from_layer)]

    def anc_copy(j, to_layer, to_col, from_layer, from_col):
        place = anc_place(j, from_layer, from_col)
        return pltpu.make_async_remote_copy(
            src_ref=place, dst_ref=place,
            send_sem=anc_send.at[j * devices + to_layer * n_col + to_col],
            recv_sem=anc_recv.at[j * devices + from_layer * n_col + from_col],
            device_id=(to_layer, row, to_col), device_id_type=MESH,
        )

    def pass_copy(j, from_layer, from_col):
        place = anc_place(j, from_layer, from_col)
        return pltpu.make_async_remote_copy(
            src_ref=place, dst_ref=place,
            send_sem=pass_send.at[j * devices + from_layer * n_col + from_col],
            recv_sem=anc_recv.at[j * devices + from_layer * n_col + from_col],
            device_id=(layer, row, partner), device_id_type=MESH,
        )

    inverse = inv_v[...]
    for j in range(chunks):
        remain = rhs_t[pl.ds(pl.multiple_of(j * span + layer * share, share), share), :] - held[j, half, inside(layer)]
        for dl, dh in group:
            from_layer, from_col = peer(dl, dh)
            part_copy(j, layer, col, from_layer, from_col).wait_recv()
            remain = remain - part_in[j, from_layer * n_col + from_col].astype(jnp.float32)
        high = remain.astype(jnp.bfloat16)
        rest = remain - high.astype(jnp.float32)
        middle = rest.astype(jnp.bfloat16)
        low = (rest - middle.astype(jnp.float32)).astype(jnp.bfloat16)
        solved = dot_last(high, inverse) + (dot_last(middle, inverse) + dot_last(low, inverse))
        anc_t[j, col, inside(layer)] = solved.astype(jnp.bfloat16)
        for dl, dh in reversed(group):
            anc_copy(j, *peer(dl, dh), layer, col).start()
        pass_copy(j, layer, col).start()

    def fold_copy(j, to_row, from_row):
        return pltpu.make_async_remote_copy(
            src_ref=fold.at[j, to_row], dst_ref=fold_in.at[j, from_row],
            send_sem=fold_send.at[j * n_row + to_row], recv_sem=fold_recv.at[j * n_row + from_row],
            device_id=(layer, to_row, col), device_id_type=MESH,
        )

    blocks_down = upper_v.shape[0] // block
    for j in range(chunks):
        for dl, dh in group:
            from_layer, from_col = peer(dl, dh)
            anc_copy(j, layer, col, from_layer, from_col).wait_recv()
            pass_copy(j, from_layer, from_col).start()
        totals = [None] * blocks_down
        for parity in (side, other):
            for dh in range(halves):
                from_col = lax.rem(half + dh, halves) * 2 + parity
                if parity is other:
                    for from_layer in range(n_layer):
                        pass_copy(j, from_layer, from_col).wait_recv()
                for i in range(blocks_down):
                    tile = upper_v[i * block:(i + 1) * block, pl.ds(pl.multiple_of(from_col * block, block), block)]
                    term = dot_last(tile, anc_t[j, from_col]) * upper_mask[i, from_col].astype(jnp.float32)
                    totals[i] = term if totals[i] is None else totals[i] + term
        for i in range(blocks_down):
            fold[j, i * strips:(i + 1) * strips] = totals[i].astype(jnp.bfloat16).reshape(strips, strip, span)
        for dr in range(1, n_row):
            fold_copy(j, lax.rem(row + dr, n_row), row).start()

    for j in range(chunks):
        anc_out[:, j * span:(j + 1) * span] = anc_t[j, col].T
    for j in range(chunks):
        correct = fold[j, row].astype(jnp.float32)
        for dr in range(1, n_row):
            from_row = lax.rem(row + dr, n_row)
            fold_copy(j, row, from_row).wait_recv()
            correct = correct + fold_in[j, from_row].astype(jnp.float32)
        columns = slice(j * span, (j + 1) * span)
        new_leaves[0, :, columns] = (leaf_v[:, columns].astype(jnp.float32) - correct).astype(jnp.bfloat16)

    for dr in range(1, n_row):
        for j in range(chunks):
            x_copy(j, lax.rem(row + dr, n_row), row).wait_send()
            fold_copy(j, lax.rem(row + dr, n_row), row).wait_send()
    for j in range(chunks):
        for h in range(halves):
            pair_copy(j, h).wait_send()
        pass_copy(j, layer, col).wait_send()
        for dl, dh in group:
            to_layer, to_col = peer(dl, dh)
            part_copy(j, to_layer, to_col, layer, col).wait_send()
            anc_copy(j, to_layer, to_col, layer, col).wait_send()
            pass_copy(j, to_layer, to_col).wait_send()


def finish(leaves, anc, leaves_out, anc_out, sem):
    copies = [
        pltpu.make_async_copy(anc, anc_out, sem.at[0]),
        pltpu.make_async_copy(leaves, leaves_out, sem.at[1]),
    ]
    for copy in copies:
        copy.start()
    for copy in copies:
        copy.wait()


def shards(n_layer, n_row, n_col, leaf_sol, lower_blocks, lower_mask, upper_blocks, upper_mask, anc_rhs, diag_inv):
    block = diag_inv.shape[1]
    width = leaf_sol.shape[2]
    strip = leaf_sol.shape[1]
    chunks = 2
    span = width // chunks
    share = span // n_layer
    halves = n_col // 2
    bf16, f32 = jnp.bfloat16, jnp.float32
    anywhere = pl.BlockSpec(memory_space=pltpu.HBM)
    scalars = pl.BlockSpec(memory_space=pltpu.SMEM)
    vmem = pl.BlockSpec(memory_space=pltpu.VMEM)
    devices = n_layer * n_col
    dma = lambda *sizes: [pltpu.SemaphoreType.DMA((size,)) for size in sizes]
    out_shape = (
        jax.ShapeDtypeStruct(leaf_sol.shape, bf16),
        jax.ShapeDtypeStruct(anc_rhs.shape, bf16),
    )
    results = pl.pallas_call(
        functools.partial(kernel, n_layer, n_row, n_col, chunks),
        out_shape=(pltpu.VMEM(leaf_sol.shape, bf16), pltpu.VMEM(anc_rhs.shape, bf16)),
        in_specs=[anywhere, anywhere, scalars, anywhere, scalars, anywhere, anywhere],
        out_specs=(vmem, vmem),
        scratch_shapes=[
            pltpu.VMEM((strip, width), bf16),
            pltpu.VMEM(lower_blocks.shape, bf16),
            pltpu.VMEM(upper_blocks.shape, bf16),
            pltpu.VMEM(anc_rhs.shape, bf16),
            pltpu.VMEM(diag_inv.shape, bf16),
            pltpu.VMEM((chunks, n_row, strip, span), bf16),
            pltpu.VMEM((chunks, n_row * strip // block, span, block), bf16),
            pltpu.VMEM((width, block), f32),
            pltpu.VMEM((chunks, halves, span, block), bf16),
            pltpu.VMEM((chunks, halves, span, block), bf16),
            pltpu.VMEM((chunks, halves, span, block), f32),
            pltpu.VMEM((chunks, halves, span, block), bf16),
            pltpu.VMEM((chunks, devices, share, block), bf16),
            pltpu.VMEM((chunks, n_col, span, block), bf16),
            pltpu.VMEM((chunks, n_row, strip, span), bf16),
            pltpu.VMEM((chunks, n_row, strip, span), bf16),
            *dma(
                5, chunks * n_row, chunks * n_row, chunks * halves, chunks * halves,
                *[chunks * devices] * 5, chunks * n_row, chunks * n_row,
            ),
        ],
        compiler_params=pltpu.CompilerParams(
            collective_id=0, has_side_effects=True,
        ),
    )(leaf_sol, lower_blocks, lower_mask.T, upper_blocks, upper_mask, anc_rhs, diag_inv)
    anyplace = pl.BlockSpec(memory_space=pl.ANY)
    return pl.pallas_call(
        finish,
        out_shape=out_shape,
        in_specs=[anyplace] * 2,
        out_specs=(anyplace, anyplace),
        scratch_shapes=dma(2),
        compiler_params=pltpu.CompilerParams(vmem_limit_bytes=1024 * 1024),
    )(*results)


def solution(mesh):
    in_specs = (
        P(("layer", "col"), "row", None),
        P(("layer", "row"), "col"),
        P(("layer", "row"), "col"),
        P(("layer", "col"), "row"),
        P(("layer", "col"), "row"),
        P(("row", "col"), None),
        P(("row", "col"), None),
    )
    out_specs = (P(("layer", "col"), "row", None), P(("row", "col"), None))
    body = functools.partial(shards, mesh.shape["layer"], mesh.shape["row"], mesh.shape["col"])
    return jax.shard_map(body, mesh=mesh, in_specs=in_specs, out_specs=out_specs, check_vma=False)
```

```python
import functools

import jax
import jax.numpy as jnp
from jax import lax
from jax.experimental import pallas as pl
from jax.experimental.pallas import tpu as pltpu
from jax.sharding import PartitionSpec as P

MESH = pl.DeviceIdType.MESH


def dot_last(a, b):
    return lax.dot_general(a, b, (((1,), (1,)), ((), ())), preferred_element_type=jnp.float32)


def kernel(
    n_layer, n_row, n_col, chunks, subs,
    leaf, lower, lower_mask, upper, upper_mask, rhs, inv,
    new_leaves, anc_out,
    leaf_v, lower_v, upper_v, rhs_v, inv_v, x_all, x_t, rhs_t,
    pair_out, pair_in, held, part, part_in, anc_t, fold, fold_in,
    local_sem, x_send, x_recv, pair_send, pair_recv, part_send, part_recv,
    anc_send, pass_send, anc_recv, fold_send, fold_recv,
):
    layer = lax.axis_index("layer")
    row = lax.axis_index("row")
    col = lax.axis_index("col")
    halves = n_col // 2
    half, side = col // 2, lax.rem(col, 2)
    other = 1 - side
    partner = half * 2 + other
    block = inv_v.shape[0]
    width = rhs_v.shape[1]
    span = width // chunks
    share = span // n_layer
    piece = share // subs
    strip = leaf_v.shape[0]
    depth = n_row * strip
    devices = n_layer * n_col
    group = [(dl, dh) for dl in range(n_layer) for dh in range(halves) if (dl, dh) != (0, 0)]

    def peer(dl, dh):
        return lax.rem(layer + dl, n_layer), lax.rem(half + dh, halves) * 2 + side

    loads = [
        pltpu.make_async_copy(source, target, local_sem.at[index])
        for index, (source, target) in enumerate(
            ((leaf.at[0], leaf_v), (lower, lower_v), (rhs, rhs_v), (inv, inv_v), (upper, upper_v))
        )
    ]
    for load in loads:
        load.start()

    barrier = pltpu.get_barrier_semaphore()
    for dr in reversed(range(1, n_row)):
        pl.semaphore_signal(barrier, inc=1, device_id=(layer, lax.rem(row + dr, n_row), col), device_id_type=MESH)
    for dl, dh in group:
        to_layer, to_col = peer(dl, dh)
        pl.semaphore_signal(barrier, inc=1, device_id=(to_layer, row, to_col), device_id_type=MESH)
    pl.semaphore_signal(barrier, inc=1, device_id=(layer, row, partner), device_id_type=MESH)
    pl.semaphore_wait(barrier, n_row + len(group))

    def x_copy(j, to_row, from_row):
        return pltpu.make_async_remote_copy(
            src_ref=leaf.at[0, :, pl.ds(j * span, span)], dst_ref=x_all.at[j, from_row],
            send_sem=x_send.at[j * n_row + to_row], recv_sem=x_recv.at[j * n_row + from_row],
            device_id=(layer, to_row, col), device_id_type=MESH,
        )

    for j in range(chunks):
        for dr in range(1, n_row):
            x_copy(j, lax.rem(row + dr, n_row), row).start()
    loads[0].wait()
    for j in range(chunks):
        x_all[j, row] = leaf_v[:, j * span:(j + 1) * span]
    loads[2].wait()
    rhs_t[...] = rhs_v[...].astype(jnp.float32).T
    loads[1].wait()
    loads[3].wait()
    loads[4].wait()
    strips = block // strip

    def partial_sum(j, to_col):
        total = None
        for k in range(depth // block):
            rows = lower_v[pl.ds(pl.multiple_of(to_col * block, block), block), k * block:(k + 1) * block]
            term = dot_last(x_t[j, k], rows) * lower_mask[k, to_col].astype(jnp.float32)
            total = term if total is None else total + term
        return total

    def pair_copy(j, h):
        return pltpu.make_async_remote_copy(
            src_ref=pair_out.at[j, h], dst_ref=pair_in.at[j, h],
            send_sem=pair_send.at[j * halves + h], recv_sem=pair_recv.at[j * halves + h],
            device_id=(layer, row, partner), device_id_type=MESH,
        )

    def portion(index, s):
        return pl.ds(pl.multiple_of(index * share + s * piece, piece), piece)

    def part_copy(j, s, to_layer, to_col, from_layer, from_col):
        base = (j * subs + s) * devices
        return pltpu.make_async_remote_copy(
            src_ref=part.at[j, to_col // 2, portion(to_layer, s)],
            dst_ref=part_in.at[j, s, from_layer * n_col + from_col],
            send_sem=part_send.at[base + to_layer * n_col + to_col],
            recv_sem=part_recv.at[base + from_layer * n_col + from_col],
            device_id=(to_layer, row, to_col), device_id_type=MESH,
        )

    for j in range(chunks):
        for dr in range(1, n_row):
            x_copy(j, row, lax.rem(row + dr, n_row)).wait_recv()
        for k in range(depth // block):
            x_t[j, k] = x_all[j, k * strips:(k + 1) * strips].reshape(block, span).T
        for h in range(halves):
            pair_out[j, h] = partial_sum(j, h * 2 + other).astype(jnp.bfloat16)
            pair_copy(j, h).start()
        for h in range(halves):
            held[j, h] = partial_sum(j, h * 2 + side)
        for h in range(halves):
            pair_copy(j, h).wait_recv()
            total = held[j, h] + pair_in[j, h].astype(jnp.float32)
            held[j, h] = total
            part[j, h] = total.astype(jnp.bfloat16)
        for s in range(subs):
            for dl, dh in reversed(group):
                part_copy(j, s, *peer(dl, dh), layer, col).start()

    def anc_place(j, s, from_layer, from_col):
        return anc_t.at[j, from_col, portion(from_layer, s)]

    def anc_copy(j, s, to_layer, to_col, from_layer, from_col):
        place = anc_place(j, s, from_layer, from_col)
        base = (j * subs + s) * devices
        return pltpu.make_async_remote_copy(
            src_ref=place, dst_ref=place,
            send_sem=anc_send.at[base + to_layer * n_col + to_col],
            recv_sem=anc_recv.at[base + from_layer * n_col + from_col],
            device_id=(to_layer, row, to_col), device_id_type=MESH,
        )

    def pass_copy(j, s, from_layer, from_col):
        place = anc_place(j, s, from_layer, from_col)
        base = (j * subs + s) * devices
        return pltpu.make_async_remote_copy(
            src_ref=place, dst_ref=place,
            send_sem=pass_send.at[base + from_layer * n_col + from_col],
            recv_sem=anc_recv.at[base + from_layer * n_col + from_col],
            device_id=(layer, row, partner), device_id_type=MESH,
        )

    inverse = inv_v[...]
    for j in range(chunks):
        for s in range(subs):
            own = portion(layer, s)
            place = pl.ds(pl.multiple_of(j * span + layer * share + s * piece, piece), piece)
            remain = rhs_t[place, :] - held[j, half, own]
            for dl, dh in group:
                from_layer, from_col = peer(dl, dh)
                part_copy(j, s, layer, col, from_layer, from_col).wait_recv()
                remain = remain - part_in[j, s, from_layer * n_col + from_col].astype(jnp.float32)
            high = remain.astype(jnp.bfloat16)
            rest = remain - high.astype(jnp.float32)
            middle = rest.astype(jnp.bfloat16)
            low = (rest - middle.astype(jnp.float32)).astype(jnp.bfloat16)
            terms = dot_last(jnp.concatenate([high, middle, low], axis=0), inverse)
            solved = terms[:piece] + (terms[piece:2 * piece] + terms[2 * piece:])
            anc_t[j, col, own] = solved.astype(jnp.bfloat16)
            for dl, dh in reversed(group):
                anc_copy(j, s, *peer(dl, dh), layer, col).start()
            pass_copy(j, s, layer, col).start()

    def fold_copy(j, to_row, from_row):
        return pltpu.make_async_remote_copy(
            src_ref=fold.at[j, to_row], dst_ref=fold_in.at[j, from_row],
            send_sem=fold_send.at[j * n_row + to_row], recv_sem=fold_recv.at[j * n_row + from_row],
            device_id=(layer, to_row, col), device_id_type=MESH,
        )

    blocks_down = upper_v.shape[0] // block
    for j in range(chunks):
        for s in range(subs):
            for dl, dh in group:
                from_layer, from_col = peer(dl, dh)
                anc_copy(j, s, layer, col, from_layer, from_col).wait_recv()
                pass_copy(j, s, from_layer, from_col).start()
        totals = [None] * blocks_down
        for parity in (side, other):
            for dh in range(halves):
                from_col = lax.rem(half + dh, halves) * 2 + parity
                if parity is other:
                    for s in range(subs):
                        for from_layer in range(n_layer):
                            pass_copy(j, s, from_layer, from_col).wait_recv()
                for i in range(blocks_down):
                    tile = upper_v[i * block:(i + 1) * block, pl.ds(pl.multiple_of(from_col * block, block), block)]
                    term = dot_last(tile, anc_t[j, from_col]) * upper_mask[i, from_col].astype(jnp.float32)
                    totals[i] = term if totals[i] is None else totals[i] + term
        for i in range(blocks_down):
            fold[j, i * strips:(i + 1) * strips] = totals[i].astype(jnp.bfloat16).reshape(strips, strip, span)
        for dr in range(1, n_row):
            fold_copy(j, lax.rem(row + dr, n_row), row).start()

    for j in range(chunks):
        anc_out[:, j * span:(j + 1) * span] = anc_t[j, col].T
    for j in range(chunks):
        correct = fold[j, row].astype(jnp.float32)
        for dr in range(1, n_row):
            from_row = lax.rem(row + dr, n_row)
            fold_copy(j, row, from_row).wait_recv()
            correct = correct + fold_in[j, from_row].astype(jnp.float32)
        columns = slice(j * span, (j + 1) * span)
        new_leaves[0, :, columns] = (leaf_v[:, columns].astype(jnp.float32) - correct).astype(jnp.bfloat16)

    for dr in range(1, n_row):
        for j in range(chunks):
            x_copy(j, lax.rem(row + dr, n_row), row).wait_send()
            fold_copy(j, lax.rem(row + dr, n_row), row).wait_send()
    for j in range(chunks):
        for h in range(halves):
            pair_copy(j, h).wait_send()
        for s in range(subs):
            pass_copy(j, s, layer, col).wait_send()
            for dl, dh in group:
                to_layer, to_col = peer(dl, dh)
                part_copy(j, s, to_layer, to_col, layer, col).wait_send()
                anc_copy(j, s, to_layer, to_col, layer, col).wait_send()
                pass_copy(j, s, to_layer, to_col).wait_send()


def finish(leaves, anc, leaves_out, anc_out, sem):
    copies = [
        pltpu.make_async_copy(anc, anc_out, sem.at[0]),
        pltpu.make_async_copy(leaves, leaves_out, sem.at[1]),
    ]
    for copy in copies:
        copy.start()
    for copy in copies:
        copy.wait()


def shards(n_layer, n_row, n_col, leaf_sol, lower_blocks, lower_mask, upper_blocks, upper_mask, anc_rhs, diag_inv):
    block = diag_inv.shape[1]
    width = leaf_sol.shape[2]
    strip = leaf_sol.shape[1]
    chunks = 2
    span = width // chunks
    share = span // n_layer
    subs = 2 if share >= 32 else 1
    halves = n_col // 2
    bf16, f32 = jnp.bfloat16, jnp.float32
    anywhere = pl.BlockSpec(memory_space=pltpu.HBM)
    scalars = pl.BlockSpec(memory_space=pltpu.SMEM)
    vmem = pl.BlockSpec(memory_space=pltpu.VMEM)
    devices = n_layer * n_col
    dma = lambda *sizes: [pltpu.SemaphoreType.DMA((size,)) for size in sizes]
    out_shape = (
        jax.ShapeDtypeStruct(leaf_sol.shape, bf16),
        jax.ShapeDtypeStruct(anc_rhs.shape, bf16),
    )
    results = pl.pallas_call(
        functools.partial(kernel, n_layer, n_row, n_col, chunks, subs),
        out_shape=(pltpu.VMEM(leaf_sol.shape, bf16), pltpu.VMEM(anc_rhs.shape, bf16)),
        in_specs=[anywhere, anywhere, scalars, anywhere, scalars, anywhere, anywhere],
        out_specs=(vmem, vmem),
        scratch_shapes=[
            pltpu.VMEM((strip, width), bf16),
            pltpu.VMEM(lower_blocks.shape, bf16),
            pltpu.VMEM(upper_blocks.shape, bf16),
            pltpu.VMEM(anc_rhs.shape, bf16),
            pltpu.VMEM(diag_inv.shape, bf16),
            pltpu.VMEM((chunks, n_row, strip, span), bf16),
            pltpu.VMEM((chunks, n_row * strip // block, span, block), bf16),
            pltpu.VMEM((width, block), f32),
            pltpu.VMEM((chunks, halves, span, block), bf16),
            pltpu.VMEM((chunks, halves, span, block), bf16),
            pltpu.VMEM((chunks, halves, span, block), f32),
            pltpu.VMEM((chunks, halves, span, block), bf16),
            pltpu.VMEM((chunks, subs, devices, share // subs, block), bf16),
            pltpu.VMEM((chunks, n_col, span, block), bf16),
            pltpu.VMEM((chunks, n_row, strip, span), bf16),
            pltpu.VMEM((chunks, n_row, strip, span), bf16),
            *dma(
                5, chunks * n_row, chunks * n_row, chunks * halves, chunks * halves,
                *[chunks * subs * devices] * 5, chunks * n_row, chunks * n_row,
            ),
        ],
        compiler_params=pltpu.CompilerParams(
            collective_id=0, has_side_effects=True,
        ),
    )(leaf_sol, lower_blocks, lower_mask.T, upper_blocks, upper_mask, anc_rhs, diag_inv)
    anyplace = pl.BlockSpec(memory_space=pl.ANY)
    return pl.pallas_call(
        finish,
        out_shape=out_shape,
        in_specs=[anyplace] * 2,
        out_specs=(anyplace, anyplace),
        scratch_shapes=dma(2),
        compiler_params=pltpu.CompilerParams(vmem_limit_bytes=1024 * 1024),
    )(*results)


def solution(mesh):
    in_specs = (
        P(("layer", "col"), "row", None),
        P(("layer", "row"), "col"),
        P(("layer", "row"), "col"),
        P(("layer", "col"), "row"),
        P(("layer", "col"), "row"),
        P(("row", "col"), None),
        P(("row", "col"), None),
    )
    out_specs = (P(("layer", "col"), "row", None), P(("row", "col"), None))
    body = functools.partial(shards, mesh.shape["layer"], mesh.shape["row"], mesh.shape["col"])
    return jax.shard_map(body, mesh=mesh, in_specs=in_specs, out_specs=out_specs, check_vma=False)
```

```python
import functools

import jax
import jax.numpy as jnp
from jax import lax
from jax.experimental import pallas as pl
from jax.experimental.pallas import tpu as pltpu
from jax.sharding import PartitionSpec as P

MESH = pl.DeviceIdType.MESH


def dot_last(a, b):
    return lax.dot_general(a, b, (((1,), (1,)), ((), ())), preferred_element_type=jnp.float32)


def kernel(
    n_layer, n_row, n_col, chunks,
    leaf, lower, lower_marks, upper, upper_marks, rhs, inv,
    new_leaves, anc_out,
    lower_mask, upper_mask, leaf_v, lower_v, upper_v, rhs_v, inv_v, x_all, x_t, rhs_t,
    pair_out, pair_in, held, part, part_in, anc_t, fold, fold_in,
    local_sem, x_send, x_recv, pair_send, pair_recv, part_send, part_recv,
    anc_send, pass_send, anc_recv, fold_send, fold_recv,
):
    layer = lax.axis_index("layer")
    row = lax.axis_index("row")
    col = lax.axis_index("col")
    halves = n_col // 2
    half, side = col // 2, lax.rem(col, 2)
    other = 1 - side
    partner = half * 2 + other
    block = inv_v.shape[0]
    width = rhs_v.shape[1]
    span = width // chunks
    share = span // n_layer
    strip = leaf_v.shape[0]
    depth = n_row * strip
    devices = n_layer * n_col
    group = [(dl, dh) for dl in range(n_layer) for dh in range(halves) if (dl, dh) != (0, 0)]

    def peer(dl, dh):
        return lax.rem(layer + dl, n_layer), lax.rem(half + dh, halves) * 2 + side

    barrier = pltpu.get_barrier_semaphore()
    for dr in reversed(range(1, n_row)):
        pl.semaphore_signal(barrier, inc=1, device_id=(layer, lax.rem(row + dr, n_row), col), device_id_type=MESH)
    for dl, dh in group:
        to_layer, to_col = peer(dl, dh)
        pl.semaphore_signal(barrier, inc=1, device_id=(to_layer, row, to_col), device_id_type=MESH)
    pl.semaphore_signal(barrier, inc=1, device_id=(layer, row, partner), device_id_type=MESH)
    loads = [
        pltpu.make_async_copy(source, target, local_sem.at[index])
        for index, (source, target) in enumerate(
            (
                (leaf.at[0], leaf_v), (lower, lower_v), (rhs, rhs_v), (inv, inv_v), (upper, upper_v),
                (lower_marks, lower_mask), (upper_marks, upper_mask),
            )
        )
    ]
    for load in loads:
        load.start()
    loads[0].wait()
    pl.semaphore_wait(barrier, n_row + len(group))

    def x_copy(j, to_row, from_row):
        return pltpu.make_async_remote_copy(
            src_ref=leaf_v.at[:, pl.ds(j * span, span)], dst_ref=x_all.at[j, from_row],
            send_sem=x_send.at[j * n_row + to_row], recv_sem=x_recv.at[j * n_row + from_row],
            device_id=(layer, to_row, col), device_id_type=MESH,
        )

    for j in range(chunks):
        for dr in range(1, n_row):
            x_copy(j, lax.rem(row + dr, n_row), row).start()
    for j in range(chunks):
        x_all[j, row] = leaf_v[:, j * span:(j + 1) * span]
    loads[2].wait()
    rhs_t[...] = rhs_v[...].astype(jnp.float32).T
    loads[1].wait()
    loads[3].wait()
    for load in loads[4:]:
        load.wait()
    strips = block // strip

    def partial_sum(j, to_col):
        total = None
        for k in range(depth // block):
            rows = lower_v[pl.ds(pl.multiple_of(to_col * block, block), block), k * block:(k + 1) * block]
            term = dot_last(x_t[j, k], rows) * lower_mask[k, to_col].astype(jnp.float32)
            total = term if total is None else total + term
        return total

    def pair_copy(j, h):
        return pltpu.make_async_remote_copy(
            src_ref=pair_out.at[j, h], dst_ref=pair_in.at[j, h],
            send_sem=pair_send.at[j * halves + h], recv_sem=pair_recv.at[j * halves + h],
            device_id=(layer, row, partner), device_id_type=MESH,
        )

    def inside(index):
        return pl.ds(pl.multiple_of(index * share, share), share)

    def part_copy(j, to_layer, to_col, from_layer, from_col):
        return pltpu.make_async_remote_copy(
            src_ref=part.at[j, to_col // 2, inside(to_layer)],
            dst_ref=part_in.at[j, from_layer * n_col + from_col],
            send_sem=part_send.at[j * devices + to_layer * n_col + to_col],
            recv_sem=part_recv.at[j * devices + from_layer * n_col + from_col],
            device_id=(to_layer, row, to_col), device_id_type=MESH,
        )

    for j in range(chunks):
        for dr in range(1, n_row):
            x_copy(j, row, lax.rem(row + dr, n_row)).wait_recv()
        for k in range(depth // block):
            x_t[j, k] = x_all[j, k * strips:(k + 1) * strips].reshape(block, span).T
        for h in range(halves):
            pair_out[j, h] = partial_sum(j, h * 2 + other).astype(jnp.bfloat16)
            pair_copy(j, h).start()
        for h in range(halves):
            held[j, h] = partial_sum(j, h * 2 + side)
        for h in range(halves):
            pair_copy(j, h).wait_recv()
            total = held[j, h] + pair_in[j, h].astype(jnp.float32)
            held[j, h] = total
            part[j, h] = total.astype(jnp.bfloat16)
        for dl, dh in reversed(group):
            part_copy(j, *peer(dl, dh), layer, col).start()

    def anc_place(j, from_layer, from_col):
        return anc_t.at[j, from_col, inside(from_layer)]

    def anc_copy(j, to_layer, to_col, from_layer, from_col):
        place = anc_place(j, from_layer, from_col)
        return pltpu.make_async_remote_copy(
            src_ref=place, dst_ref=place,
            send_sem=anc_send.at[j * devices + to_layer * n_col + to_col],
            recv_sem=anc_recv.at[j * devices + from_layer * n_col + from_col],
            device_id=(to_layer, row, to_col), device_id_type=MESH,
        )

    def pass_copy(j, from_layer, from_col):
        place = anc_place(j, from_layer, from_col)
        return pltpu.make_async_remote_copy(
            src_ref=place, dst_ref=place,
            send_sem=pass_send.at[j * devices + from_layer * n_col + from_col],
            recv_sem=anc_recv.at[j * devices + from_layer * n_col + from_col],
            device_id=(layer, row, partner), device_id_type=MESH,
        )

    inverse = inv_v[...]
    for j in range(chunks):
        remain = rhs_t[pl.ds(pl.multiple_of(j * span + layer * share, share), share), :] - held[j, half, inside(layer)]
        for dl, dh in group:
            from_layer, from_col = peer(dl, dh)
            part_copy(j, layer, col, from_layer, from_col).wait_recv()
            remain = remain - part_in[j, from_layer * n_col + from_col].astype(jnp.float32)
        high = remain.astype(jnp.bfloat16)
        rest = remain - high.astype(jnp.float32)
        middle = rest.astype(jnp.bfloat16)
        low = (rest - middle.astype(jnp.float32)).astype(jnp.bfloat16)
        solved = dot_last(high, inverse) + (dot_last(middle, inverse) + dot_last(low, inverse))
        anc_t[j, col, inside(layer)] = solved.astype(jnp.bfloat16)
        for dl, dh in reversed(group):
            anc_copy(j, *peer(dl, dh), layer, col).start()
        pass_copy(j, layer, col).start()

    def fold_copy(j, to_row, from_row):
        return pltpu.make_async_remote_copy(
            src_ref=fold.at[j, to_row], dst_ref=fold_in.at[j, from_row],
            send_sem=fold_send.at[j * n_row + to_row], recv_sem=fold_recv.at[j * n_row + from_row],
            device_id=(layer, to_row, col), device_id_type=MESH,
        )

    blocks_down = upper_v.shape[0] // block
    for j in range(chunks):
        for dl, dh in group:
            from_layer, from_col = peer(dl, dh)
            anc_copy(j, layer, col, from_layer, from_col).wait_recv()
            pass_copy(j, from_layer, from_col).start()
        totals = [None] * blocks_down
        for parity in (side, other):
            for dh in range(halves):
                from_col = lax.rem(half + dh, halves) * 2 + parity
                if parity is other:
                    for from_layer in range(n_layer):
                        pass_copy(j, from_layer, from_col).wait_recv()
                for i in range(blocks_down):
                    tile = upper_v[i * block:(i + 1) * block, pl.ds(pl.multiple_of(from_col * block, block), block)]
                    term = dot_last(tile, anc_t[j, from_col]) * upper_mask[i, from_col].astype(jnp.float32)
                    totals[i] = term if totals[i] is None else totals[i] + term
        for i in range(blocks_down):
            fold[j, i * strips:(i + 1) * strips] = totals[i].astype(jnp.bfloat16).reshape(strips, strip, span)
        for dr in range(1, n_row):
            fold_copy(j, lax.rem(row + dr, n_row), row).start()

    for j in range(chunks):
        anc_out[:, j * span:(j + 1) * span] = anc_t[j, col].T
    for j in range(chunks):
        correct = fold[j, row].astype(jnp.float32)
        for dr in range(1, n_row):
            from_row = lax.rem(row + dr, n_row)
            fold_copy(j, row, from_row).wait_recv()
            correct = correct + fold_in[j, from_row].astype(jnp.float32)
        columns = slice(j * span, (j + 1) * span)
        new_leaves[0, :, columns] = (leaf_v[:, columns].astype(jnp.float32) - correct).astype(jnp.bfloat16)

    for dr in range(1, n_row):
        for j in range(chunks):
            x_copy(j, lax.rem(row + dr, n_row), row).wait_send()
            fold_copy(j, lax.rem(row + dr, n_row), row).wait_send()
    for j in range(chunks):
        for h in range(halves):
            pair_copy(j, h).wait_send()
        pass_copy(j, layer, col).wait_send()
        for dl, dh in group:
            to_layer, to_col = peer(dl, dh)
            part_copy(j, to_layer, to_col, layer, col).wait_send()
            anc_copy(j, to_layer, to_col, layer, col).wait_send()
            pass_copy(j, to_layer, to_col).wait_send()


def finish(leaves, anc, leaves_out, anc_out, sem):
    copies = [
        pltpu.make_async_copy(anc, anc_out, sem.at[0]),
        pltpu.make_async_copy(leaves, leaves_out, sem.at[1]),
    ]
    for copy in copies:
        copy.start()
    for copy in copies:
        copy.wait()


def shards(n_layer, n_row, n_col, leaf_sol, lower_blocks, lower_mask, upper_blocks, upper_mask, anc_rhs, diag_inv):
    block = diag_inv.shape[1]
    width = leaf_sol.shape[2]
    strip = leaf_sol.shape[1]
    chunks = 2
    span = width // chunks
    share = span // n_layer
    halves = n_col // 2
    bf16, f32 = jnp.bfloat16, jnp.float32
    anywhere = pl.BlockSpec(memory_space=pltpu.HBM)
    lower_marks = lower_mask.T
    vmem = pl.BlockSpec(memory_space=pltpu.VMEM)
    devices = n_layer * n_col
    dma = lambda *sizes: [pltpu.SemaphoreType.DMA((size,)) for size in sizes]
    out_shape = (
        jax.ShapeDtypeStruct(leaf_sol.shape, bf16),
        jax.ShapeDtypeStruct(anc_rhs.shape, bf16),
    )
    results = pl.pallas_call(
        functools.partial(kernel, n_layer, n_row, n_col, chunks),
        out_shape=(pltpu.VMEM(leaf_sol.shape, bf16), pltpu.VMEM(anc_rhs.shape, bf16)),
        in_specs=[anywhere] * 7,
        out_specs=(vmem, vmem),
        scratch_shapes=[
            pltpu.SMEM(lower_marks.shape, jnp.int32),
            pltpu.SMEM(upper_mask.shape, jnp.int32),
            pltpu.VMEM((strip, width), bf16),
            pltpu.VMEM(lower_blocks.shape, bf16),
            pltpu.VMEM(upper_blocks.shape, bf16),
            pltpu.VMEM(anc_rhs.shape, bf16),
            pltpu.VMEM(diag_inv.shape, bf16),
            pltpu.VMEM((chunks, n_row, strip, span), bf16),
            pltpu.VMEM((chunks, n_row * strip // block, span, block), bf16),
            pltpu.VMEM((width, block), f32),
            pltpu.VMEM((chunks, halves, span, block), bf16),
            pltpu.VMEM((chunks, halves, span, block), bf16),
            pltpu.VMEM((chunks, halves, span, block), f32),
            pltpu.VMEM((chunks, halves, span, block), bf16),
            pltpu.VMEM((chunks, devices, share, block), bf16),
            pltpu.VMEM((chunks, n_col, span, block), bf16),
            pltpu.VMEM((chunks, n_row, strip, span), bf16),
            pltpu.VMEM((chunks, n_row, strip, span), bf16),
            *dma(
                7, chunks * n_row, chunks * n_row, chunks * halves, chunks * halves,
                *[chunks * devices] * 5, chunks * n_row, chunks * n_row,
            ),
        ],
        compiler_params=pltpu.CompilerParams(
            collective_id=0, has_side_effects=True,
        ),
    )(leaf_sol, lower_blocks, lower_marks, upper_blocks, upper_mask, anc_rhs, diag_inv)
    anyplace = pl.BlockSpec(memory_space=pl.ANY)
    return pl.pallas_call(
        finish,
        out_shape=out_shape,
        in_specs=[anyplace] * 2,
        out_specs=(anyplace, anyplace),
        scratch_shapes=dma(2),
        compiler_params=pltpu.CompilerParams(vmem_limit_bytes=1024 * 1024),
    )(*results)


def solution(mesh):
    in_specs = (
        P(("layer", "col"), "row", None),
        P(("layer", "row"), "col"),
        P(("layer", "row"), "col"),
        P(("layer", "col"), "row"),
        P(("layer", "col"), "row"),
        P(("row", "col"), None),
        P(("row", "col"), None),
    )
    out_specs = (P(("layer", "col"), "row", None), P(("row", "col"), None))
    body = functools.partial(shards, mesh.shape["layer"], mesh.shape["row"], mesh.shape["col"])
    return jax.shard_map(body, mesh=mesh, in_specs=in_specs, out_specs=out_specs, check_vma=False)
```

```python
import functools

import jax
import jax.numpy as jnp
from jax import lax
from jax.experimental import pallas as pl
from jax.experimental.pallas import tpu as pltpu
from jax.sharding import PartitionSpec as P

MESH = pl.DeviceIdType.MESH


def dot_last(a, b):
    return lax.dot_general(a, b, (((1,), (1,)), ((), ())), preferred_element_type=jnp.float32)


def kernel(
    n_layer, n_row, n_col, chunks,
    leaf, lower, lower_marks, upper, upper_marks, rhs, inv,
    new_leaves, anc_out,
    lower_mask, upper_mask, leaf_v, lower_v, upper_v, rhs_v, inv_v, x_all, x_t, rhs_t,
    pair_out, pair_in, held, part, part_in, anc_t, fold, fold_in,
    local_sem, x_send, x_recv, pair_send, pair_recv, part_send, part_recv,
    anc_send, pass_send, anc_recv, fold_send, fold_recv,
):
    layer = lax.axis_index("layer")
    row = lax.axis_index("row")
    col = lax.axis_index("col")
    halves = n_col // 2
    half, side = col // 2, lax.rem(col, 2)
    other = 1 - side
    partner = half * 2 + other
    block = inv_v.shape[0]
    width = rhs_v.shape[1]
    span = width // chunks
    share = span // n_layer
    strip = leaf_v.shape[0]
    depth = n_row * strip
    devices = n_layer * n_col
    group = [(dl, dh) for dl in range(n_layer) for dh in range(halves) if (dl, dh) != (0, 0)]

    def peer(dl, dh):
        return lax.rem(layer + dl, n_layer), lax.rem(half + dh, halves) * 2 + side

    barrier = pltpu.get_barrier_semaphore()
    for dr in reversed(range(1, n_row)):
        pl.semaphore_signal(barrier, inc=1, device_id=(layer, lax.rem(row + dr, n_row), col), device_id_type=MESH)
    for dl, dh in group:
        to_layer, to_col = peer(dl, dh)
        pl.semaphore_signal(barrier, inc=1, device_id=(to_layer, row, to_col), device_id_type=MESH)
    pl.semaphore_signal(barrier, inc=1, device_id=(layer, row, partner), device_id_type=MESH)
    loads = [
        pltpu.make_async_copy(source, target, local_sem.at[index])
        for index, (source, target) in enumerate(
            (
                (leaf.at[0], leaf_v), (lower, lower_v), (rhs, rhs_v), (inv, inv_v), (upper, upper_v),
                (lower_marks, lower_mask), (upper_marks, upper_mask),
            )
        )
    ]
    for load in loads:
        load.start()
    loads[0].wait()
    pl.semaphore_wait(barrier, n_row + len(group))

    def x_copy(j, to_row, from_row):
        return pltpu.make_async_remote_copy(
            src_ref=leaf_v.at[:, pl.ds(j * span, span)], dst_ref=x_all.at[j, from_row],
            send_sem=x_send.at[j * n_row + to_row], recv_sem=x_recv.at[j * n_row + from_row],
            device_id=(layer, to_row, col), device_id_type=MESH,
        )

    for j in range(chunks):
        for dr in range(1, n_row):
            x_copy(j, lax.rem(row + dr, n_row), row).start()
    for j in range(chunks):
        x_all[j, row] = leaf_v[:, j * span:(j + 1) * span]
    loads[2].wait()
    rhs_t[...] = rhs_v[...].astype(jnp.float32).T
    loads[1].wait()
    loads[3].wait()
    for load in loads[4:]:
        load.wait()
    strips = block // strip

    def partial_sum(j, to_col):
        total = None
        for k in range(depth // block):
            rows = lower_v[pl.ds(pl.multiple_of(to_col * block, block), block), k * block:(k + 1) * block]
            term = dot_last(x_t[j, k], rows) * lower_mask[k, to_col].astype(jnp.float32)
            total = term if total is None else total + term
        return total

    def pair_copy(j, h):
        return pltpu.make_async_remote_copy(
            src_ref=pair_out.at[j, h], dst_ref=pair_in.at[j, h],
            send_sem=pair_send.at[j * halves + h], recv_sem=pair_recv.at[j * halves + h],
            device_id=(layer, row, partner), device_id_type=MESH,
        )

    def inside(index):
        return pl.ds(pl.multiple_of(index * share, share), share)

    def part_copy(j, to_layer, to_col, from_layer, from_col):
        return pltpu.make_async_remote_copy(
            src_ref=part.at[j, to_col // 2, inside(to_layer)],
            dst_ref=part_in.at[j, from_layer * n_col + from_col],
            send_sem=part_send.at[j * devices + to_layer * n_col + to_col],
            recv_sem=part_recv.at[j * devices + from_layer * n_col + from_col],
            device_id=(to_layer, row, to_col), device_id_type=MESH,
        )

    for j in range(chunks):
        for dr in range(1, n_row):
            x_copy(j, row, lax.rem(row + dr, n_row)).wait_recv()
        for k in range(depth // block):
            x_t[j, k] = x_all[j, k * strips:(k + 1) * strips].reshape(block, span).T
        turns = [(dh, lax.rem(half + dh, halves)) for dh in reversed(range(halves))]
        for _, h in turns:
            pair_out[j, h] = partial_sum(j, h * 2 + other).astype(jnp.bfloat16)
            pair_copy(j, h).start()
        for _, h in turns:
            held[j, h] = partial_sum(j, h * 2 + side)
        for turn, h in turns:
            pair_copy(j, h).wait_recv()
            total = held[j, h] + pair_in[j, h].astype(jnp.float32)
            held[j, h] = total
            part[j, h] = total.astype(jnp.bfloat16)
            for dl, dh in reversed(group):
                if dh == turn:
                    part_copy(j, *peer(dl, dh), layer, col).start()

    def anc_place(j, from_layer, from_col):
        return anc_t.at[j, from_col, inside(from_layer)]

    def anc_copy(j, to_layer, to_col, from_layer, from_col):
        place = anc_place(j, from_layer, from_col)
        return pltpu.make_async_remote_copy(
            src_ref=place, dst_ref=place,
            send_sem=anc_send.at[j * devices + to_layer * n_col + to_col],
            recv_sem=anc_recv.at[j * devices + from_layer * n_col + from_col],
            device_id=(to_layer, row, to_col), device_id_type=MESH,
        )

    def pass_copy(j, from_layer, from_col):
        place = anc_place(j, from_layer, from_col)
        return pltpu.make_async_remote_copy(
            src_ref=place, dst_ref=place,
            send_sem=pass_send.at[j * devices + from_layer * n_col + from_col],
            recv_sem=anc_recv.at[j * devices + from_layer * n_col + from_col],
            device_id=(layer, row, partner), device_id_type=MESH,
        )

    inverse = inv_v[...]
    for j in range(chunks):
        remain = rhs_t[pl.ds(pl.multiple_of(j * span + layer * share, share), share), :] - held[j, half, inside(layer)]
        for dl, dh in group:
            from_layer, from_col = peer(dl, dh)
            part_copy(j, layer, col, from_layer, from_col).wait_recv()
            remain = remain - part_in[j, from_layer * n_col + from_col].astype(jnp.float32)
        high = remain.astype(jnp.bfloat16)
        rest = remain - high.astype(jnp.float32)
        middle = rest.astype(jnp.bfloat16)
        low = (rest - middle.astype(jnp.float32)).astype(jnp.bfloat16)
        terms = dot_last(jnp.concatenate([high, middle, low], axis=0), inverse)
        solved = terms[:share] + (terms[share:2 * share] + terms[2 * share:])
        anc_t[j, col, inside(layer)] = solved.astype(jnp.bfloat16)
        for dl, dh in reversed(group):
            anc_copy(j, *peer(dl, dh), layer, col).start()
        pass_copy(j, layer, col).start()

    def fold_copy(j, to_row, from_row):
        return pltpu.make_async_remote_copy(
            src_ref=fold.at[j, to_row], dst_ref=fold_in.at[j, from_row],
            send_sem=fold_send.at[j * n_row + to_row], recv_sem=fold_recv.at[j * n_row + from_row],
            device_id=(layer, to_row, col), device_id_type=MESH,
        )

    blocks_down = upper_v.shape[0] // block
    for j in range(chunks):
        for dl, dh in group:
            from_layer, from_col = peer(dl, dh)
            anc_copy(j, layer, col, from_layer, from_col).wait_recv()
            pass_copy(j, from_layer, from_col).start()
        totals = [None] * blocks_down
        for parity in (side, other):
            for dh in range(halves):
                from_col = lax.rem(half + dh, halves) * 2 + parity
                if parity is other:
                    for from_layer in range(n_layer):
                        pass_copy(j, from_layer, from_col).wait_recv()
                for i in range(blocks_down):
                    tile = upper_v[i * block:(i + 1) * block, pl.ds(pl.multiple_of(from_col * block, block), block)]
                    term = dot_last(tile, anc_t[j, from_col]) * upper_mask[i, from_col].astype(jnp.float32)
                    totals[i] = term if totals[i] is None else totals[i] + term
        for i in range(blocks_down):
            fold[j, i * strips:(i + 1) * strips] = totals[i].astype(jnp.bfloat16).reshape(strips, strip, span)
        for dr in range(1, n_row):
            fold_copy(j, lax.rem(row + dr, n_row), row).start()

    for j in range(chunks):
        anc_out[:, j * span:(j + 1) * span] = anc_t[j, col].T
    for j in range(chunks):
        correct = fold[j, row].astype(jnp.float32)
        for dr in range(1, n_row):
            from_row = lax.rem(row + dr, n_row)
            fold_copy(j, row, from_row).wait_recv()
            correct = correct + fold_in[j, from_row].astype(jnp.float32)
        columns = slice(j * span, (j + 1) * span)
        new_leaves[0, :, columns] = (leaf_v[:, columns].astype(jnp.float32) - correct).astype(jnp.bfloat16)

    for dr in range(1, n_row):
        for j in range(chunks):
            x_copy(j, lax.rem(row + dr, n_row), row).wait_send()
            fold_copy(j, lax.rem(row + dr, n_row), row).wait_send()
    for j in range(chunks):
        for h in range(halves):
            pair_copy(j, h).wait_send()
        pass_copy(j, layer, col).wait_send()
        for dl, dh in group:
            to_layer, to_col = peer(dl, dh)
            part_copy(j, to_layer, to_col, layer, col).wait_send()
            anc_copy(j, to_layer, to_col, layer, col).wait_send()
            pass_copy(j, to_layer, to_col).wait_send()


def finish(leaves, anc, leaves_out, anc_out, sem):
    copies = [
        pltpu.make_async_copy(anc, anc_out, sem.at[0]),
        pltpu.make_async_copy(leaves, leaves_out, sem.at[1]),
    ]
    for copy in copies:
        copy.start()
    for copy in copies:
        copy.wait()


def shards(n_layer, n_row, n_col, leaf_sol, lower_blocks, lower_mask, upper_blocks, upper_mask, anc_rhs, diag_inv):
    block = diag_inv.shape[1]
    width = leaf_sol.shape[2]
    strip = leaf_sol.shape[1]
    chunks = 2
    span = width // chunks
    share = span // n_layer
    halves = n_col // 2
    bf16, f32 = jnp.bfloat16, jnp.float32
    anywhere = pl.BlockSpec(memory_space=pltpu.HBM)
    lower_marks = lower_mask.T
    vmem = pl.BlockSpec(memory_space=pltpu.VMEM)
    devices = n_layer * n_col
    dma = lambda *sizes: [pltpu.SemaphoreType.DMA((size,)) for size in sizes]
    out_shape = (
        jax.ShapeDtypeStruct(leaf_sol.shape, bf16),
        jax.ShapeDtypeStruct(anc_rhs.shape, bf16),
    )
    results = pl.pallas_call(
        functools.partial(kernel, n_layer, n_row, n_col, chunks),
        out_shape=(pltpu.VMEM(leaf_sol.shape, bf16), pltpu.VMEM(anc_rhs.shape, bf16)),
        in_specs=[anywhere] * 7,
        out_specs=(vmem, vmem),
        scratch_shapes=[
            pltpu.SMEM(lower_marks.shape, jnp.int32),
            pltpu.SMEM(upper_mask.shape, jnp.int32),
            pltpu.VMEM((strip, width), bf16),
            pltpu.VMEM(lower_blocks.shape, bf16),
            pltpu.VMEM(upper_blocks.shape, bf16),
            pltpu.VMEM(anc_rhs.shape, bf16),
            pltpu.VMEM(diag_inv.shape, bf16),
            pltpu.VMEM((chunks, n_row, strip, span), bf16),
            pltpu.VMEM((chunks, n_row * strip // block, span, block), bf16),
            pltpu.VMEM((width, block), f32),
            pltpu.VMEM((chunks, halves, span, block), bf16),
            pltpu.VMEM((chunks, halves, span, block), bf16),
            pltpu.VMEM((chunks, halves, span, block), f32),
            pltpu.VMEM((chunks, halves, span, block), bf16),
            pltpu.VMEM((chunks, devices, share, block), bf16),
            pltpu.VMEM((chunks, n_col, span, block), bf16),
            pltpu.VMEM((chunks, n_row, strip, span), bf16),
            pltpu.VMEM((chunks, n_row, strip, span), bf16),
            *dma(
                7, chunks * n_row, chunks * n_row, chunks * halves, chunks * halves,
                *[chunks * devices] * 5, chunks * n_row, chunks * n_row,
            ),
        ],
        compiler_params=pltpu.CompilerParams(
            collective_id=0, has_side_effects=True,
        ),
    )(leaf_sol, lower_blocks, lower_marks, upper_blocks, upper_mask, anc_rhs, diag_inv)
    anyplace = pl.BlockSpec(memory_space=pl.ANY)
    return pl.pallas_call(
        finish,
        out_shape=out_shape,
        in_specs=[anyplace] * 2,
        out_specs=(anyplace, anyplace),
        scratch_shapes=dma(2),
        compiler_params=pltpu.CompilerParams(vmem_limit_bytes=1024 * 1024),
    )(*results)


def solution(mesh):
    in_specs = (
        P(("layer", "col"), "row", None),
        P(("layer", "row"), "col"),
        P(("layer", "row"), "col"),
        P(("layer", "col"), "row"),
        P(("layer", "col"), "row"),
        P(("row", "col"), None),
        P(("row", "col"), None),
    )
    out_specs = (P(("layer", "col"), "row", None), P(("row", "col"), None))
    body = functools.partial(shards, mesh.shape["layer"], mesh.shape["row"], mesh.shape["col"])
    return jax.shard_map(body, mesh=mesh, in_specs=in_specs, out_specs=out_specs, check_vma=False)
```
